256 devices in a mesh: row: 16 (over z, core), col: 4 (over x), rhs: 4 (over y).
Axes of the slice: x: 4, y: 4, z: 8, core: 2. Of those that a mesh axis runs over, the one named last changes fastest.
Arguments:
- factor: bfloat16 [32768, 8192], P('row', 'col'), may hold values from -0.0625 to 0.0625
- samples: float32 [32768, 512], P('row', 'rhs'), may hold values from -6 to 6
- inverses: bfloat16 [8, 1024, 1024], P(None, 'row', 'col'), may hold values from -0.1875 to 0.1875
Outputs:
- solution: bfloat16 [8, 1024, 512], P(None, 'col', 'rhs')
- remaining: float32 [32768, 512], P(('row', 'col'), 'rhs')
The draws below stay inside these ranges and needn't reach their ends.
All inputs are finite; a program needn't handle non-finite values.
Results may differ from the reference program's by a relative error of at most 0.006.
Values may be sent and summed in bfloat16 or wider, within the bound.
No kernel may reach another device: no remote copies, remote signals or barrier semaphores. Data moves between devices by JAX's collectives and lax.ppermute only.
A program may use at most 64 MiB of HBM per device.

```python
import jax
import jax.numpy as jnp

NB = 1024
NDIAG = 8
NBR = 32
S = 512
N_ROW = 16
N_COL = 4


def level_of(own_key, shape, split, low, largest):
    def one(position, shards_of):
        steps = jax.random.uniform(jax.random.fold_in(jax.random.fold_in(own_key, 6), position), (shards_of,), jnp.float32, low / len(split), largest / len(split))
        return jnp.repeat(jnp.exp(steps), shape[position] // shards_of).reshape((-1,) + (1,) * (len(shape) - position - 1))

    factor_of = one(*split[0])
    for cut in split[1:]:
        factor_of = factor_of * one(*cut)
    return factor_of


def noise(own_key, shape, spread, reach, cuts=(), kind=jnp.bfloat16):
    values = jax.random.normal(own_key, shape, jnp.float32) * spread
    if len(cuts) > 0:
        values = level_of(own_key, shape, cuts, -0.22, 0.18) * values
    return jnp.clip(values, min=-reach, max=reach).astype(kind)


def setup_inputs(seed: int = 0) -> dict:
    key_of = jax.random.split(jax.random.key(seed), 4)
    return {
        "factor": noise(key_of[0], (NBR * NB, NDIAG * NB), (NDIAG * NB) ** -0.5, 0.0625, ((0, 16), (1, 4))),
        "samples": noise(key_of[1], (NBR * NB, S), 1.0, 6.0, ((0, 16), (1, 4)), jnp.float32),
        "inverses": noise(key_of[2], (NDIAG, NB, NB), NB ** -0.5, 0.1875, ((1, 16), (2, 4))),
    }


def reference(factor, samples, inverses):
    block_rows = factor.shape[0] // NB
    row_slots = block_rows // N_ROW
    col_slots = NDIAG // N_COL
    stored_ids = jnp.arange(block_rows)
    factor_rows = (stored_ids % row_slots) * N_ROW + stored_ids // row_slots
    remaining = samples
    solutions = []
    for block in range(NDIAG):
        stored = (block % N_ROW) * row_slots + block // N_ROW
        lowered = remaining[stored * NB:(stored + 1) * NB].astype(jnp.bfloat16)
        solved = jnp.dot(jnp.tril(inverses[block]), lowered, preferred_element_type=jnp.float32).astype(jnp.bfloat16)
        solutions.append(solved)
        stored_col = (block % N_COL) * col_slots + block // N_COL
        column = factor[:, stored_col * NB:(stored_col + 1) * NB]
        update = jnp.dot(column, solved, preferred_element_type=jnp.float32)
        below_mask = jnp.repeat(factor_rows > block, NB)
        remaining = remaining - jnp.where(below_mask[:, None], update, jnp.float32(0.0))
    return jnp.stack(solutions), remaining
```

```python
import jax
import jax.numpy as jnp
from jax import lax
from jax.sharding import PartitionSpec as P

ROWS = 16
COLS = 4
DIAG = 8
HOME = (0, 0, 1, 1, 3, 3, 1, 1)


def at(row, col):
    return (row % ROWS) * COLS + col % COLS


def send(value, pairs):
    return lax.ppermute(value, ("row", "col"), [(at(*a), at(*b)) for a, b in pairs])


def mul(a, b):
    return jnp.dot(a, b, preferred_element_type=jnp.float32)


def shards(factor, samples, inverses):
    row = lax.axis_index("row")
    col = lax.axis_index("col")
    nb = inverses.shape[1] * ROWS
    q = nb // COLS
    bf = jnp.bfloat16
    slot0 = factor[:nb, :nb]
    slot1 = factor[:nb, nb:]
    rhs = samples[:nb]

    slab = inverses.shape[1]
    keep = (row * slab + jnp.arange(slab))[:, None] >= (col * q + jnp.arange(q))[None, :]
    slabs = jnp.where(keep[None], inverses, jnp.zeros((), bf))
    padded = jnp.concatenate([slabs, jnp.zeros((ROWS - DIAG,) + slabs.shape[1:], bf)])
    column_part = lax.all_to_all(padded, "row", 0, 0, tiled=True).reshape(nb, q)
    parts = []
    for k in range(COLS):
        pairs = [((i, k), (i, HOME[i])) for i in range(DIAG) if HOME[i] != k]
        got = send(column_part[k * q :], pairs)
        got = got + jnp.where(col == k, column_part[k * q :], jnp.zeros((), bf))
        parts.append(jnp.pad(got, ((k * q, 0), (0, 0))))
    inverse = jnp.concatenate(parts, axis=1)

    early = row < 4
    diag_low = send(jnp.where(early, slot0, slot1), [((3, 2), (3, 1)), ((5, 0), (5, 3)), ((7, 2), (7, 1))])
    moved_two = send(
        jnp.where(row < 6, slot0, slot1),
        [((4, 2), (4, 3)), ((5, 2), (5, 3)), ((6, 0), (6, 1)), ((7, 0), (7, 1))],
    )

    x0 = mul(inverse, rhs.astype(bf)).astype(bf)
    a0 = send(x0, [((0, 0), (1, 0))])
    p1 = rhs - mul(slot0, a0)
    x1 = mul(inverse, p1.astype(bf)).astype(bf)
    mine = jnp.where(row == 0, x0, x1)

    b1 = send(mine, [((0, 0), (2, 0)), ((1, 0), (2, 1))])
    c1 = send(b1, [((2, 0), (3, 0))])
    u1 = mul(slot0, b1 + c1)
    s1 = send(u1.astype(bf), [((2, 0), (2, 1)), ((3, 0), (3, 1))])
    acc = rhs - s1.astype(jnp.float32)
    p2 = acc - u1
    x2 = mul(inverse, p2.astype(bf)).astype(bf)
    a1 = send(jnp.concatenate([b1, x2]), [((2, 1), (3, 1))])
    p3 = acc - mul(slot0, a1[:nb]) - mul(diag_low, a1[nb:])
    x3 = mul(inverse, p3.astype(bf)).astype(bf)
    mine = jnp.where(row == 2, x2, mine)
    d2 = send(mine, [((2, 1), (4, 3)), ((0, 0), (4, 0)), ((1, 0), (4, 1))])
    b2 = send(x3, [((3, 1), (4, 3))])
    mine = jnp.where(row == 3, x3, mine)

    d2 = d2 + send(d2, [((4, 0), (5, 0)), ((4, 1), (5, 1)), ((4, 3), (5, 3))])
    zero = jnp.zeros((), bf)
    u2 = mul(slot0, jnp.where(col == 3, zero, d2)) + mul(moved_two, jnp.where(col == 3, d2, zero))
    w2 = u2.astype(bf)
    s2 = [send(w2, [((4, k), (4, 3)), ((5, k), (5, 3))]) for k in (0, 1)]
    acc = rhs - u2 - s2[0].astype(jnp.float32) - s2[1].astype(jnp.float32)
    p4 = acc - mul(slot0, b2)
    x4 = mul(inverse, p4.astype(bf)).astype(bf)
    a2 = send(jnp.concatenate([b2, x4]), [((4, 3), (5, 3))])
    p5 = acc - mul(slot0, a2[:nb]) - mul(diag_low, a2[nb:])
    x5 = mul(inverse, p5.astype(bf)).astype(bf)
    far = send(mine, [((0, 0), (6, 0)), ((1, 0), (6, 1)), ((2, 1), (6, 2)), ((3, 1), (6, 3))])
    d3 = send(x4, [((4, 3), (6, 1))])
    b3 = send(x5, [((5, 3), (6, 1))])

    far = far + send(far, [((6, k), (7, k)) for k in range(COLS)])
    u3 = mul(slot0, far)
    w3 = u3.astype(bf)
    s3 = [send(w3, [((6, k), (6, 1)), ((7, k), (7, 1))]) for k in (0, 2, 3)]
    d3 = d3 + send(d3, [((6, 1), (7, 1))])
    acc = rhs - u3 - sum(s.astype(jnp.float32) for s in s3) - mul(moved_two, d3)
    p6 = acc - mul(slot1, b3)
    x6 = mul(inverse, p6.astype(bf)).astype(bf)
    a3 = send(jnp.concatenate([b3, x6]), [((6, 1), (7, 1))])
    p7 = acc - mul(slot1, a3[:nb]) - mul(diag_low, a3[nb:])
    x7 = mul(inverse, p7.astype(bf)).astype(bf)

    x = mine
    p = jnp.where(row == 0, rhs, p1)
    for i, (xi, pi) in enumerate(((x2, p2), (x3, p3), (x4, p4), (x5, p5), (x6, p6), (x7, p7)), 2):
        x = jnp.where(row == i, xi, x)
        p = jnp.where(row == i, pi, p)
    home = jnp.asarray(HOME + (COLS,) * (ROWS - DIAG), jnp.int32)[row]
    here = col == home

    quarter = jnp.where(here, lax.dynamic_slice_in_dim(x, col * q, q, 0), zero)
    for s in range(1, COLS):
        piece = lax.dynamic_slice_in_dim(x, ((col + s) % COLS) * q, q, 0)
        quarter = quarter + send(piece, [((i, HOME[i]), (i, HOME[i] + s)) for i in range(DIAG)])
    solved = lax.all_gather(quarter, "row", axis=0, tiled=False)[:DIAG]
    full = lax.all_to_all(solved.reshape(2, COLS, q, -1), "col", 1, 1, tiled=True).reshape(2 * nb, -1)
    total = mul(factor, full)
    top = jnp.where(row < DIAG, jnp.where(here, rhs - p, jnp.float32(0)), total[:nb])
    total = jnp.concatenate([top, total[nb:]]).astype(bf)
    total = lax.all_to_all(total.reshape(COLS, 2 * nb // COLS, -1), "col", 0, 0, tiled=True)
    total = jnp.sum(total.astype(jnp.float32), axis=0)
    out_rows = 2 * nb // COLS
    return solved, lax.dynamic_slice_in_dim(samples, col * out_rows, out_rows, 0) - total


def solution(mesh):
    in_specs = (P("row", "col"), P("row", "rhs"), P(None, "row", "col"))
    out_specs = (P(None, "col", "rhs"), P(("row", "col"), "rhs"))
    return jax.shard_map(shards, mesh=mesh, in_specs=in_specs, out_specs=out_specs, check_vma=False)
```
